32 devices in a mesh: mic: 8 (over z, x), orient: 4 (over y, core).
Axes of the slice: x: 2, y: 2, z: 4, core: 2. Of those that a mesh axis runs over, the one named last changes fastest.
Arguments:
- micrograph: bfloat16 [3072, 384], P('mic'), may hold values from -6 to 6
- search_spectra: bfloat16 [64, 384, 768], P('orient', 'mic'), may hold values from -6 to 6
- refine_spectra: bfloat16 [8, 32, 384, 768], P('mic', 'orient'), may hold values from -6 to 6
- ctf: float32 [384, 384], replicated, may hold values from -1 to 1
- ref_owner: int32 [128, 1], P(('mic', 'orient')), may hold values from 0 to 3; in each aligned block of 4 rows (0 to 3, 4 to 7, ...) at most 2 rows name the same one
- ref_slot: int32 [128, 1], P(('mic', 'orient')), may hold values from 0 to 7
Outputs:
- peak_map: float32 [3072, 384], P('mic')
- mean_map: float32 [3072, 384], P('mic')
- scaled_peak: float32 [3072, 384], P('mic')
- refined_map: float32 [3072, 384], P('mic')
The draws below stay inside these ranges and needn't reach their ends.
Inputs may be any that keep to these rules, and one draw needn't show every extreme that they name: `ref_owner`: in each aligned block of 4 rows (the list entries of one micrograph that one orientation block handles) no owner is named more than 2 times, and in some blocks one owner is named exactly 2 times.
All inputs are finite; a program needn't handle non-finite values.
Results may differ from the reference program's by a relative error of at most 0.0086.
Values may be sent and summed in bfloat16 or wider, within the bound.
A program may use at most 128 MiB of HBM per device.

```python
import math
import jax
import jax.numpy as jnp
import numpy as np
from jax import lax

P_SIZE = 384
RB = 8
RD = 4
CAP = 2
MICS = 8
NS = 64
RSET = 32
RL = 16
N_ORIENT = 4


def with_ends(drawn, own_key, low, high):
    longest = drawn.shape.index(max(drawn.shape))
    spots = []
    for shift in (0, 1):
        where = [jax.random.randint(jax.random.fold_in(own_key, axis), (), 0, length) for axis, length in enumerate(drawn.shape)]
        where[longest] = (where[longest] + shift) % drawn.shape[longest]
        spots.append(tuple(where))
    return drawn.at[spots[0]].set(low).at[spots[1]].set(high)


def block_scale(key, extent, cuts, smallest, high):
    gain = 1.0
    for dim, blocks in cuts:
        heights = jax.random.uniform(jax.random.fold_in(jax.random.fold_in(key, 6), dim), (blocks,), jnp.float32, smallest / len(cuts), high / len(cuts))
        gain = gain * jnp.repeat(jnp.exp(heights), extent[dim] // blocks).reshape((-1,) + (1,) * (len(extent) - 1 - dim))
    return gain


def shared_out(key, own, number, rows, amount, top, bound, lean):
    ranking = jax.random.permutation(key, amount)
    packed, usual = shares(amount, rows * top, bound, lean, True), shares(amount, rows * top, bound, lean, False)
    places = jnp.arange(amount)

    def named(tallies, rotation):
        used = int((tallies > 0).sum())
        fixed = max(1, used // 4)
        shifted = fixed + (places - fixed + rotation * (used - fixed)) % max(1, amount - fixed)
        return jnp.zeros((amount,), jnp.int32).at[ranking[jnp.where(places < fixed, places, shifted)]].set(jnp.asarray(tallies, jnp.int32))

    tallies = jnp.where(number % 4 == 0, named(packed, number // 4), named(usual, number - number // 4 - 1))
    mixed = jax.random.permutation(jax.random.fold_in(own, 3), amount)
    giver, receiver = mixed[0:amount // 2 * 2:2], mixed[1:amount // 2 * 2:2]
    margin = jnp.minimum(tallies[giver] - 1, bound - tallies[receiver]) // 2
    margin = jnp.where((giver == ranking[0]) | (receiver == ranking[0]) | (tallies[receiver] == 0), 0, jnp.maximum(margin, 0))
    shifted = jax.random.randint(jax.random.fold_in(own, 4), (amount // 2,), 0, 1 << 20) % (margin + 1)
    tallies = tallies.at[giver].add(-shifted).at[receiver].add(shifted)
    items = jnp.searchsorted(jnp.cumsum(tallies), jnp.arange(rows * top), side="right").astype(jnp.int32)
    table = items.reshape(top, rows).T
    table = table[jax.random.permutation(jax.random.fold_in(own, 1), rows)]
    rotation = jax.random.randint(jax.random.fold_in(own, 2), (rows, 1), 0, top)
    return jnp.take_along_axis(table, (jnp.arange(top)[None, :] + rotation) % top, axis=1)


def shares(number_of, total, most, slope, full):
    weights = [(1 << 20) // math.isqrt(grade ** slope) + 1 for grade in range(1, number_of + 1)]
    largest = most if full else min(most, max(-(-total // number_of), total * weights[0] // sum(weights)))
    least = 1 if total - largest >= number_of - 1 else 0
    counts, rest = [largest] + [least] * (number_of - 1), total - largest - least * (number_of - 1)
    while rest > 0:
        candidates = [i for i in range(1, number_of) if counts[i] < largest] or [i for i in range(1, number_of) if counts[i] < most]
        mass, budget = sum([weights[i] for i in candidates]), rest
        for i in candidates:
            more = min(most - counts[i], max(1, budget * weights[i] // mass), rest)
            counts[i] = counts[i] + more
            rest = rest - more
    return np.array(counts)


def normal_values(key, extent, width, most, split=(), kind=jnp.bfloat16):
    values = jax.random.normal(key, extent, jnp.float32) * width
    if len(split) > 0:
        values = block_scale(key, extent, split, -0.22, 0.18) * values
    return jnp.clip(values, min=-most, max=most).astype(kind)


def setup_inputs(seed: int = 0) -> dict:
    key_of = jax.random.split(jax.random.key(seed), 7)
    micrograph = normal_values(key_of[0], (MICS * P_SIZE, P_SIZE), 1.0, 6.0, ((0, 8),))
    search_spectra = normal_values(key_of[1], (NS, P_SIZE, 2 * P_SIZE), 1.0, 6.0, ((0, 4), (1, 8)))
    refine_spectra = normal_values(key_of[2], (MICS, RSET, P_SIZE, 2 * P_SIZE), 1.0, 6.0, ((0, 8), (1, 4)))
    ctf = jnp.clip(jax.random.uniform(key_of[3], (P_SIZE, P_SIZE), jnp.float32, -1.0, 1.0), -1.0, 1.0)
    ref_owner_keys = jax.random.split(jax.random.fold_in(key_of[4], 1), (MICS * RL) // RD)
    ref_owner_turns = jax.random.permutation(jax.random.fold_in(key_of[4], 3), (MICS * RL) // RD)
    ref_owner = jax.vmap(lambda own, number: shared_out(jax.random.fold_in(key_of[4], 2), own, number, RD, N_ORIENT, 1, CAP, 2))(ref_owner_keys, ref_owner_turns).reshape((MICS * RL, 1))
    ref_slot = with_ends(jax.random.randint(key_of[5], (MICS * RL, 1), 0, RB), jax.random.fold_in(key_of[5], 1), 0, RB - 1).astype(jnp.int32)
    return dict(micrograph=micrograph, search_spectra=search_spectra, refine_spectra=refine_spectra, ctf=ctf, ref_owner=ref_owner, ref_slot=ref_slot)


def make_tables(box_edge):
    positions = jnp.arange(box_edge, dtype=jnp.int32)
    products = positions[:, None] * positions[None, :] % box_edge
    angles = products.astype(jnp.float32) * (2.0 * math.pi / box_edge)
    cosine = jnp.cos(angles)
    sines = jnp.sin(angles)
    fwd_cos = cosine.astype(jnp.bfloat16)
    fwd_sin = sines.astype(jnp.bfloat16)
    inv_cos = (cosine / box_edge).astype(jnp.bfloat16)
    inv_sin = (sines / box_edge).astype(jnp.bfloat16)
    fwd_half = jnp.concatenate([fwd_cos, -fwd_sin], axis=1)
    fwd_full = jnp.stack([jnp.stack([fwd_cos, fwd_sin], -1), jnp.stack([-fwd_sin, fwd_cos], -1)], 0)
    inv_cols = jnp.concatenate([jnp.concatenate([inv_cos, inv_sin], 1), jnp.concatenate([-inv_sin, inv_cos], 1)], 0)
    inv_rows = jnp.stack([inv_cos, -inv_sin], -1)
    return (fwd_half, fwd_full, inv_cols, inv_rows)

def forward(tile_image, fwd_half, fwd_full):
    box_edge = tile_image.shape[0]
    half_spectrum = jnp.dot(tile_image, fwd_half, preferred_element_type=jnp.float32).astype(jnp.bfloat16)
    stacked = half_spectrum.reshape(box_edge, 2, box_edge)
    spectrum = jnp.einsum('dykc,kcx->ydx', fwd_full.astype(jnp.float32), stacked.astype(jnp.float32))
    return spectrum.reshape(box_edge, 2 * box_edge).astype(jnp.bfloat16)

def multiply(spectrum, filtered):
    box_edge = spectrum.shape[-1] // 2
    spec_real = spectrum[..., :box_edge].astype(jnp.float32)
    spec_imag = spectrum[..., box_edge:].astype(jnp.float32)
    filt_real = filtered[..., :box_edge].astype(jnp.float32)
    filt_imag = filtered[..., box_edge:].astype(jnp.float32)
    prod_real = spec_real * filt_real + spec_imag * filt_imag
    prod_imag = spec_imag * filt_real - spec_real * filt_imag
    return jnp.concatenate([prod_real, prod_imag], -1).astype(jnp.bfloat16)

def correlate(spectrum, filtered, inv_cols, inv_rows):
    box_edge = spectrum.shape[0]
    product = multiply(spectrum, filtered)
    halfway = jnp.einsum('trl,lm->trm', product.astype(jnp.float32), inv_cols.astype(jnp.float32)).astype(jnp.bfloat16)
    stacked = halfway.reshape(halfway.shape[0], box_edge, 2, box_edge)
    return jnp.einsum('ykc,tkcx->tyx', inv_rows.astype(jnp.float32), stacked.astype(jnp.float32))

def reference(micrograph, search_spectra, refine_spectra, ctf, ref_owner, ref_slot):
    box_edge = micrograph.shape[1]
    fwd_half, fwd_full, inv_cols, inv_rows = make_tables(box_edge)
    ctf_gain = jnp.concatenate([ctf, ctf], 1)
    search_filtered = (search_spectra.astype(jnp.float32) * ctf_gain).astype(jnp.bfloat16)
    tiles = micrograph.reshape(MICS, box_edge, box_edge)
    chosen_ids = (ref_owner[:, 0] * RB + ref_slot[:, 0]).astype(jnp.int32).reshape(MICS, RL)

    def one_tile(bundle):
        tile_image, library, chosen = bundle
        spectrum = forward(tile_image, fwd_half, fwd_full)
        correlations = correlate(spectrum, search_filtered, inv_cols, inv_rows)
        picked = jnp.take(library, chosen, axis=0)
        picked_filtered = (picked.astype(jnp.float32) * ctf_gain).astype(jnp.bfloat16)
        refined = lax.optimization_barrier(jnp.max(correlate(spectrum, picked_filtered, inv_cols, inv_rows), axis=0))
        return (lax.optimization_barrier(jnp.max(correlations, axis=0)), lax.optimization_barrier(jnp.sum(correlations, axis=0)), lax.optimization_barrier(jnp.sum(correlations * correlations, axis=0)), refined)
    peak_all, total_all, square_all, refined_all = lax.map(one_tile, (tiles, refine_spectra, chosen_ids))
    count = float(NS)
    peak_map = peak_all.reshape(MICS * box_edge, box_edge)
    mean_map = (total_all / count).reshape(MICS * box_edge, box_edge)
    scaled_peak = (peak_all * lax.rsqrt(square_all / count + 1e-05)).reshape(MICS * box_edge, box_edge)
    refined_map = refined_all.reshape(MICS * box_edge, box_edge)
    return (peak_map, mean_map, scaled_peak, refined_map)
```

```python
import math

import jax
import jax.numpy as jnp
import numpy as np
from jax import lax
from jax.experimental import pallas as pl
from jax.experimental.pallas import tpu as pltpu
from jax.sharding import PartitionSpec as P


def make_tables(box_edge):
    positions = jnp.arange(box_edge, dtype=jnp.int32)
    products = positions[:, None] * positions[None, :] % box_edge
    angles = products.astype(jnp.float32) * (2.0 * math.pi / box_edge)
    cosine = jnp.cos(angles)
    sines = jnp.sin(angles)
    fwd_cos = cosine.astype(jnp.bfloat16)
    fwd_sin = sines.astype(jnp.bfloat16)
    inv_cos = (cosine / box_edge).astype(jnp.bfloat16)
    inv_sin = (sines / box_edge).astype(jnp.bfloat16)
    fwd_half = jnp.concatenate([fwd_cos, -fwd_sin], axis=1)
    fwd_full = jnp.stack([jnp.stack([fwd_cos, fwd_sin], -1), jnp.stack([-fwd_sin, fwd_cos], -1)], 0)
    inv_cols = jnp.concatenate(
        [jnp.concatenate([inv_cos, inv_sin], 1), jnp.concatenate([-inv_sin, inv_cos], 1)], 0
    )
    inv_rows = jnp.stack([inv_cos, -inv_sin], -1)
    return (fwd_half, fwd_full, inv_cols, inv_rows)


def forward(tile_image, fwd_half, fwd_full):
    box_edge = tile_image.shape[0]
    half_spectrum = jnp.dot(tile_image, fwd_half, preferred_element_type=jnp.float32).astype(
        jnp.bfloat16
    )
    stacked = half_spectrum.reshape(box_edge, 2, box_edge)
    spectrum = jnp.einsum("dykc,kcx->ydx", fwd_full, stacked, preferred_element_type=jnp.float32)
    return spectrum.reshape(box_edge, 2 * box_edge).astype(jnp.bfloat16)


def fold_matrices(edge):
    half = edge // 2
    own = np.zeros((2 * edge, edge), np.float32)
    mirror = np.zeros((2 * edge, edge), np.float32)
    for l in range(1, half):
        own[l, l] = 1.0
        own[edge + l, half + l] = 1.0
        mirror[edge - l, l] = 1.0
        mirror[2 * edge - l, half + l] = -1.0
    own[0, 0], own[edge + half, 0] = 0.5, -0.5
    own[edge, half], own[half, half] = 0.5, 0.5
    mirror[0, 0], mirror[edge + half, 0] = 0.5, 0.5
    mirror[edge, half], mirror[half, half] = -0.5, 0.5
    return jnp.asarray(own, jnp.bfloat16), jnp.asarray(mirror, jnp.bfloat16)


def gather_half(filtered):
    count, rows, width = filtered.shape
    edge = width // 2
    mics = lax.axis_size("mic")
    own_map, mirror_map = fold_matrices(edge)
    mirrored = jnp.einsum(
        "tkc,cl->tkl", filtered, mirror_map, preferred_element_type=jnp.float32
    ).astype(jnp.bfloat16)
    flip = np.zeros((rows, rows), np.float32)
    for i in range(1, rows):
        flip[i, rows - i] = 1.0
    turned = jnp.einsum(
        "ik,tkl->til", jnp.asarray(flip, jnp.bfloat16), mirrored, preferred_element_type=jnp.float32
    ).astype(jnp.bfloat16)
    first = lax.ppermute(mirrored[:, 0, :], "mic", [(m, (mics - m) % mics) for m in range(mics)])
    rest = lax.ppermute(turned, "mic", [(m, mics - 1 - m) for m in range(mics)])
    own = jnp.einsum("tkc,cl->tkl", filtered, own_map, preferred_element_type=jnp.float32)
    row = lax.broadcasted_iota(jnp.int32, (1, rows, 1), 1)
    other = jnp.where(row == 0, first[:, None, :].astype(jnp.float32), rest.astype(jnp.float32))
    folded = (own + other).astype(jnp.bfloat16)
    if rows % 16 == 0:
        return lax.all_gather(folded, "mic", axis=0)
    return lax.all_gather(folded, "mic", axis=1, tiled=True)[None]


def search_kernel(
    e_ref, gr_ref, gi_ref, gb_ref, cs_ref, col_ref, flip_ref, peak_ref, total_ref, square_ref
):
    step = pl.program_id(0)
    edge = gr_ref.shape[0]
    half = edge // 2
    e_bf = e_ref[...].reshape(edge, edge)
    e = e_bf.astype(jnp.float32)
    es = jnp.concatenate([e[:, half:], e[:, :half]], axis=1)
    gr = gr_ref[...]
    gi = gi_ref[...]
    lane = lax.broadcasted_iota(jnp.int32, (edge, edge), 1)
    low = lane < half
    narrow = lax.broadcasted_iota(jnp.int32, (edge, 128), 1)
    dr = jnp.dot(
        flip_ref[...],
        jnp.where(narrow == 0, e[:, :128], pltpu.roll(es[:, :128], 1, 1)).astype(jnp.bfloat16),
        preferred_element_type=jnp.float32,
    )
    gbr, gbi = gb_ref[:, 0:1], gb_ref[:, 1:2]
    mr, mi = dr[:, 0:1], dr[:, 1:2]
    fix_r = gbr * mr - gbi * mi
    fix_i = gbr * mi + gbi * mr
    ge, ges = gr * e, gr * es
    he, hes = gi * e, gi * es
    top = jnp.where(low, ge, -ge) + hes
    bottom = ges + jnp.where(low, -he, he)
    at_r, at_i = lane == 0, lane == half
    top = top + jnp.where(at_r, fix_r, jnp.where(at_i, fix_i, 0.0))
    bottom = bottom + jnp.where(at_r, -fix_i, jnp.where(at_i, fix_r, 0.0))
    stacked = jnp.concatenate([top.astype(jnp.bfloat16), bottom.astype(jnp.bfloat16)], axis=0)
    v = jnp.dot(cs_ref[...], stacked, preferred_element_type=jnp.float32).astype(jnp.bfloat16)
    corr = jnp.dot(v, col_ref[...], preferred_element_type=jnp.float32)

    @pl.when(step == 0)
    def _():
        peak_ref[...] = corr
        total_ref[...] = corr
        square_ref[...] = corr * corr

    @pl.when(step > 0)
    def _():
        peak_ref[...] = jnp.maximum(peak_ref[...], corr)
        total_ref[...] += corr
        square_ref[...] += corr * corr


def search_maps(gathered, gr, gi, gb, cs, col):
    mics, count, rows, edge = gathered.shape
    flip = np.zeros((edge, edge), np.float32)
    for k in range(edge):
        flip[k, (edge - k) % edge] = 1.0
    whole = lambda a: pl.BlockSpec(a.shape, lambda t: (0, 0))
    flip = jnp.asarray(flip, jnp.bfloat16)
    out = jax.ShapeDtypeStruct((edge, edge), jnp.float32)
    return pl.pallas_call(
        search_kernel,
        grid=(count,),
        in_specs=[pl.BlockSpec((mics, 1, rows, edge), lambda t: (0, t, 0, 0))]
        + [whole(a) for a in (gr, gi, gb, cs, col, flip)],
        out_specs=[pl.BlockSpec((edge, edge), lambda t: (0, 0))] * 3,
        out_shape=[out] * 3,
        compiler_params=pltpu.CompilerParams(vmem_limit_bytes=40 * 1024 * 1024),
        cost_estimate=pl.CostEstimate(flops=count * 350000000, bytes_accessed=count * 600000, transcendentals=0),
    )(gathered, gr, gi, gb, cs, col, flip)


def refine_kernel(lib_ref, ctf_ref, g_ref, cs_ref, col_ref, wanted_ref, out_ref):
    step = pl.program_id(0)
    edge = ctf_ref.shape[0]

    @pl.when(step == 0)
    def _():
        out_ref[...] = jnp.full((edge, edge), -3.0e38, jnp.float32)

    @pl.when(wanted_ref[step] > 0)
    def _():
        gain = ctf_ref[...]
        fr = (lib_ref[0, :, :edge].astype(jnp.float32) * gain).astype(jnp.bfloat16).astype(jnp.float32)
        fi = (lib_ref[0, :, edge:].astype(jnp.float32) * gain).astype(jnp.bfloat16).astype(jnp.float32)
        gr = g_ref[:, :edge].astype(jnp.float32)
        gi = g_ref[:, edge:].astype(jnp.float32)
        zr = (gr * fr + gi * fi).astype(jnp.bfloat16)
        zi = (gi * fr - gr * fi).astype(jnp.bfloat16)
        ci, si = cs_ref[:, :edge], cs_ref[:, edge:]
        dot = lambda a, b: jnp.dot(a, b, preferred_element_type=jnp.float32)
        ur = (dot(ci, zr) - dot(si, zi)).astype(jnp.bfloat16)
        ui = (dot(si, zr) + dot(ci, zi)).astype(jnp.bfloat16)
        corr = dot(ur, col_ref[:edge]) - dot(ui, col_ref[edge:])
        out_ref[...] = jnp.maximum(out_ref[...], corr)


def refine_map(library, ctf, spectrum, cs, col, wanted):
    count, edge, width = library.shape
    whole = lambda a: pl.BlockSpec(a.shape, lambda t: (0, 0))
    return pl.pallas_call(
        refine_kernel,
        grid=(count,),
        in_specs=[pl.BlockSpec((1, edge, width), lambda t: (t, 0, 0))]
        + [whole(a) for a in (ctf, spectrum, cs, col)]
        + [pl.BlockSpec(memory_space=pltpu.SMEM)],
        out_specs=pl.BlockSpec((edge, edge), lambda t: (0, 0)),
        out_shape=jax.ShapeDtypeStruct((edge, edge), jnp.float32),
        compiler_params=pltpu.CompilerParams(vmem_limit_bytes=40 * 1024 * 1024),
        cost_estimate=pl.CostEstimate(flops=count * 700000000, bytes_accessed=count * 1200000, transcendentals=0),
    )(library, ctf, spectrum, cs, col, wanted)


def join(left, right):
    low = jnp.maximum(left[0], right[0].astype(jnp.float32))
    total = left[1] + right[1].astype(jnp.float32)
    square = left[2] + right[2].astype(jnp.float32)
    return (low, total, square, jnp.maximum(left[3], right[3].astype(jnp.float32)))


def merge(maps):
    size = lax.axis_size("orient")
    edge = maps[0].shape[0]
    half = edge // 2
    core = lax.axis_index("orient") % 2
    near = [(i, i ^ 1) for i in range(size)]
    narrow = lambda values: [a.astype(jnp.bfloat16) for a in values]
    mine = [lax.dynamic_slice_in_dim(a, core * half, half, 0) for a in maps]
    theirs = narrow(lax.dynamic_slice_in_dim(a, (1 - core) * half, half, 0) for a in maps)
    state = join(mine, lax.ppermute(jnp.stack(theirs), "orient", near))
    distance = 2
    while distance < size:
        far = [(i, i ^ distance) for i in range(size)]
        state = join(state, lax.ppermute(jnp.stack(narrow(state)), "orient", far))
        distance *= 2
    final = jnp.stack(narrow(state))
    other = lax.ppermute(final, "orient", near)
    first = jnp.where(core == 0, final, other)
    second = jnp.where(core == 0, other, final)
    return [jnp.concatenate([first[i], second[i]], 0).astype(jnp.float32) for i in range(4)]


def body(micrograph, search_spectra, refine_spectra, ctf, ref_owner, ref_slot):
    edge = micrograph.shape[1]
    half = edge // 2
    fwd_half, fwd_full, inv_cols, _ = make_tables(edge)
    ctf_gain = jnp.concatenate([ctf, ctf], 1)
    rows_owned = search_spectra.shape[1]
    first_row = lax.axis_index("mic") * rows_owned
    own_gain = lax.dynamic_slice_in_dim(ctf_gain, first_row, rows_owned, 0)
    filtered = (search_spectra.astype(jnp.float32) * own_gain).astype(jnp.bfloat16)
    gathered = gather_half(filtered)
    spectrum = forward(micrograph, fwd_half, fwd_full)

    library = refine_spectra[0]
    block_size = library.shape[0]
    ids = lax.all_gather(ref_owner[:, 0] * block_size + ref_slot[:, 0], "orient", axis=0, tiled=True)
    slots = lax.axis_index("orient") * block_size + jnp.arange(block_size, dtype=jnp.int32)
    wanted = jnp.any(slots[:, None] == ids[None, :], axis=1).astype(jnp.int32)
    cs = inv_cols[:edge]
    inv_cos, inv_sin = inv_cols[:edge, :edge], inv_cols[:edge, edge:]
    refine_cols = jnp.concatenate([inv_cos, inv_sin], 0)
    refined = refine_map(library, ctf, spectrum, cs, refine_cols, wanted)

    spec = spectrum.astype(jnp.float32)
    g_r, g_i = spec[:, :edge], spec[:, edge:]
    dc = jnp.stack([g_r[:, 0], g_i[:, 0]], 1)
    ny = jnp.stack([g_r[:, half], g_i[:, half]], 1)
    ga = (dc - ny) * 0.5
    gb = (dc + ny) * 0.5
    lane = lax.broadcasted_iota(jnp.int32, (edge, half), 1)
    h_r = jnp.where(lane == 0, ga[:, 0:1], g_r[:, :half])
    h_i = jnp.where(lane == 0, ga[:, 1:2], g_i[:, :half])
    gr = jnp.concatenate([h_r, h_r], 1)
    gi = jnp.concatenate([h_i, h_i], 1)
    row = lax.broadcasted_iota(jnp.int32, (half, edge), 0)
    sin_rows = jnp.where(row == 0, inv_cos[half : half + 1], -inv_sin[:half])
    col = jnp.concatenate([inv_cos[:half], sin_rows], 0)
    peak, total, square = search_maps(gathered, gr, gi, gb, cs, col)
    peak, total, square, refined = merge([peak, total, square, refined])
    count = float(lax.axis_size("orient") * search_spectra.shape[0])
    return (peak, total / count, peak * lax.rsqrt(square / count + 1e-05), refined)


def solution(mesh):
    in_specs = (
        P("mic", None),
        P("orient", "mic", None),
        P("mic", "orient", None, None),
        P(),
        P(("mic", "orient"), None),
        P(("mic", "orient"), None),
    )
    out_specs = (P("mic", None), P("mic", None), P("mic", None), P("mic", None))
    return jax.shard_map(body, mesh=mesh, in_specs=in_specs, out_specs=out_specs, check_vma=False)
```

```python
import functools
import math

import jax
import jax.numpy as jnp
import numpy as np
from jax import lax
from jax.experimental import pallas as pl
from jax.experimental.pallas import tpu as pltpu
from jax.sharding import PartitionSpec as P

GROUPS = 4


def make_tables(box_edge):
    positions = np.arange(box_edge, dtype=np.int32)
    products = positions[:, None] * positions[None, :] % box_edge
    angles = products.astype(np.float32) * np.float32(2.0 * math.pi / box_edge)
    cosine = np.cos(angles)
    sines = np.sin(angles)
    narrow = lambda a: a.astype(np.float32).astype(jnp.bfloat16)
    fwd_cos, fwd_sin = narrow(cosine), narrow(sines)
    inv_cos = narrow(cosine / np.float32(box_edge))
    inv_sin = narrow(sines / np.float32(box_edge))
    return (fwd_cos, fwd_sin, inv_cos, inv_sin)


def forward(tile_image, fwd_cos, fwd_sin):
    box_edge = tile_image.shape[0]
    full_map = jnp.asarray(np.concatenate([fwd_cos, fwd_sin], 1))
    halved = jnp.dot(tile_image, full_map, preferred_element_type=jnp.float32).astype(jnp.bfloat16)
    ar, ai = halved[:, :box_edge], -halved[:, box_edge:]
    stacked = jnp.concatenate(
        [jnp.concatenate([ar, ai], 1), jnp.concatenate([ai, -ar], 1)], 0
    )
    return jnp.dot(full_map, stacked, preferred_element_type=jnp.float32).astype(jnp.bfloat16)


def fold_matrices(edge):
    half = edge // 2
    mirror = np.zeros((2 * edge, edge), np.float32)
    for l in range(1, half):
        mirror[edge - l, l] = 1.0
        mirror[2 * edge - l, half + l] = -1.0
    mirror[0, 0], mirror[edge + half, 0] = 0.5, 0.5
    mirror[edge, half], mirror[half, half] = -0.5, 0.5
    row = lax.broadcasted_iota(jnp.int32, (2 * edge, edge), 0)
    col = lax.broadcasted_iota(jnp.int32, (2 * edge, edge), 1)
    own = jnp.where(row == jnp.where(col < half, col, col + half), 1.0, 0.0)
    first = jnp.where(row == 0, 0.5, jnp.where(row == edge + half, -0.5, 0.0))
    middle = jnp.where((row == edge) | (row == half), 0.5, 0.0)
    own = jnp.where(col == 0, first, jnp.where(col == half, middle, own))
    return own.astype(jnp.bfloat16), jnp.asarray(mirror, jnp.bfloat16)


def fold_half(filtered):
    count, rows, width = filtered.shape
    edge = width // 2
    mics = lax.axis_size("mic")
    own_map, mirror_map = fold_matrices(edge)
    mirrored = jnp.einsum(
        "tkc,cl->tkl", filtered, mirror_map, preferred_element_type=jnp.float32
    ).astype(jnp.bfloat16)
    flip = np.zeros((rows, rows), np.float32)
    for i in range(1, rows):
        flip[i, rows - i] = 1.0
    turned = jnp.einsum(
        "ik,tkl->til", jnp.asarray(flip, jnp.bfloat16), mirrored, preferred_element_type=jnp.float32
    ).astype(jnp.bfloat16)
    first = lax.ppermute(mirrored[:, 0, :], "mic", [(m, (mics - m) % mics) for m in range(mics)])
    rest = lax.ppermute(turned, "mic", [(m, mics - 1 - m) for m in range(mics)])
    own = jnp.einsum("tkc,cl->tkl", filtered, own_map, preferred_element_type=jnp.float32)
    row = lax.broadcasted_iota(jnp.int32, (1, rows, 1), 1)
    other = jnp.where(row == 0, first[:, None, :].astype(jnp.float32), rest.astype(jnp.float32))
    return (own + other).astype(jnp.bfloat16)


def correlate(e, gr_ref, gi_ref, gb_ref, cs_ref, col_ref, flip_ref):
    edge = gr_ref.shape[0]
    half = edge // 2
    es = jnp.concatenate([e[:, half:], e[:, :half]], axis=1)
    gr = gr_ref[...]
    gi = gi_ref[...]
    lane = lax.broadcasted_iota(jnp.int32, (edge, edge), 1)
    low = lane < half
    narrow = lax.broadcasted_iota(jnp.int32, (edge, 128), 1)
    dr = jnp.dot(
        flip_ref[...],
        jnp.where(narrow == 0, e[:, :128], pltpu.roll(es[:, :128], 1, 1)).astype(jnp.bfloat16),
        preferred_element_type=jnp.float32,
    )
    gbr, gbi = gb_ref[:, 0:1], gb_ref[:, 1:2]
    mr, mi = dr[:, 0:1], dr[:, 1:2]
    fix_r = gbr * mr - gbi * mi
    fix_i = gbr * mi + gbi * mr
    ge, ges = gr * e, gr * es
    he, hes = gi * e, gi * es
    top = jnp.where(low, ge, -ge) + hes
    bottom = ges + jnp.where(low, -he, he)
    at_r, at_i = lane == 0, lane == half
    top = top + jnp.where(at_r, fix_r, jnp.where(at_i, fix_i, 0.0))
    bottom = bottom + jnp.where(at_r, -fix_i, jnp.where(at_i, fix_r, 0.0))
    stacked = jnp.concatenate([top.astype(jnp.bfloat16), bottom.astype(jnp.bfloat16)], axis=0)
    v = jnp.dot(cs_ref[...], stacked, preferred_element_type=jnp.float32).astype(jnp.bfloat16)
    return jnp.dot(v, col_ref[...], preferred_element_type=jnp.float32)


def accumulate(corr, peak_ref, total_ref, square_ref):
    peak_ref[...] = jnp.maximum(peak_ref[...], corr)
    total_ref[...] += corr
    square_ref[...] += corr * corr


def clear(peak_ref, total_ref, square_ref):
    peak_ref[...] = jnp.full(peak_ref.shape, -3.0e38, jnp.float32)
    total_ref[...] = jnp.zeros(total_ref.shape, jnp.float32)
    square_ref[...] = jnp.zeros(square_ref.shape, jnp.float32)


def search_kernel(e_ref, *refs):
    @pl.when(pl.program_id(0) == 0)
    def _():
        clear(*refs[6:])

    edge = refs[0].shape[0]
    e = e_ref[...].reshape(edge, edge).astype(jnp.float32)
    accumulate(correlate(e, *refs[:6]), *refs[6:])


def remote_kernel(groups, mics, e_ref, *refs):
    operands, maps = refs[:6], refs[6:9]
    full, up_sem, down_sem, side_sem, near_sem, far_sem = refs[9:]
    edge = operands[0].shape[0]
    depth = mics // 2
    per = e_ref.shape[0] // groups
    me = lax.axis_index("mic")
    z, x = me // 2, me % 2
    above, below, beside = me + 2, me - 2, z * 2 + 1 - x
    has_above, has_below = z < depth - 1, z > 0
    mesh_id = pl.DeviceIdType.MESH
    barrier = pltpu.get_barrier_semaphore()

    @pl.when(has_above)
    def _():
        pl.semaphore_signal(barrier, inc=1, device_id={"mic": above}, device_id_type=mesh_id)

    @pl.when(has_below)
    def _():
        pl.semaphore_signal(barrier, inc=1, device_id={"mic": below}, device_id_type=mesh_id)

    pl.semaphore_signal(barrier, inc=1, device_id={"mic": beside}, device_id_type=mesh_id)
    full[me] = e_ref[...]
    clear(*maps)

    peers = 1 + has_above.astype(jnp.int32) + has_below.astype(jnp.int32)
    pl.semaphore_wait(barrier, peers)

    def copy(group, source, column, send_sem, recv_sem, target):
        piece = full.at[source * 2 + column, pl.ds(group * per, per)]
        slot = group * depth + source
        return pltpu.make_async_remote_copy(
            src_ref=piece,
            dst_ref=piece,
            send_sem=send_sem.at[slot],
            recv_sem=recv_sem.at[slot],
            device_id={"mic": target},
            device_id_type=mesh_id,
        )

    go_up = lambda g, source: copy(g, source, x, up_sem, near_sem, above)
    go_down = lambda g, source: copy(g, source, x, down_sem, near_sem, below)
    go_side = lambda g, source: copy(g, source, x, side_sem, far_sem, beside)
    from_side = lambda g, source: copy(g, source, 1 - x, side_sem, far_sem, beside)

    for step in range(groups + depth):
        for hop in range(depth):
            g = step - hop
            if g < 0 or g >= groups:
                continue
            if hop == 0:

                @pl.when(has_above)
                def _(g=g):
                    go_up(g, z).start()

                @pl.when(has_below)
                def _(g=g):
                    go_down(g, z).start()

                go_side(g, z).start()
                continue

            @pl.when(z - hop >= 0)
            def _(g=g, hop=hop):
                go_up(g, z - hop).wait_recv()

                @pl.when(has_above)
                def _():
                    go_up(g, z - hop).start()

                go_side(g, z - hop).start()

            @pl.when(z + hop < depth)
            def _(g=g, hop=hop):
                go_down(g, z + hop).wait_recv()

                @pl.when(has_below)
                def _():
                    go_down(g, z + hop).start()

                go_side(g, z + hop).start()

        g = step - depth
        if g >= 0:
            for source in range(depth):
                from_side(g, source).wait_recv()

            def one(t, carry):
                e = full[:, t].reshape(edge, edge).astype(jnp.float32)
                accumulate(correlate(e, *operands), *maps)
                return carry

            lax.fori_loop(g * per, (g + 1) * per, one, 0)

    for g in range(groups):
        for source in range(depth):
            go_side(g, source).wait_send()

            @pl.when(jnp.logical_and(has_above, z >= source))
            def _(g=g, source=source):
                go_up(g, source).wait_send()

            @pl.when(jnp.logical_and(has_below, z <= source))
            def _(g=g, source=source):
                go_down(g, source).wait_send()


def search_maps(folded, gr, gi, gb, cs, col):
    count, rows, edge = folded.shape
    mics = lax.axis_size("mic")
    place = lambda axis: lax.broadcasted_iota(jnp.int32, (edge, edge), axis)
    flip = ((place(0) + place(1)) % edge == 0).astype(jnp.bfloat16)
    whole = lambda a: pl.BlockSpec(a.shape, lambda t: (0, 0))
    out = jax.ShapeDtypeStruct((edge, edge), jnp.float32)
    cost = pl.CostEstimate(
        flops=count * 350000000, bytes_accessed=count * 600000, transcendentals=0
    )
    if rows % 16 == 0 and mics % 2 == 0:
        groups = GROUPS if count % GROUPS == 0 else 1
        slots = groups * (mics // 2)
        vmem = pl.BlockSpec(memory_space=pltpu.VMEM)
        return pl.pallas_call(
            functools.partial(remote_kernel, groups, mics),
            in_specs=[vmem] * 7,
            out_specs=[vmem] * 3,
            out_shape=[out] * 3,
            scratch_shapes=[pltpu.VMEM((mics, count, rows, edge), jnp.bfloat16)]
            + [pltpu.SemaphoreType.DMA((slots,))] * 5,
            compiler_params=pltpu.CompilerParams(
                vmem_limit_bytes=40 * 1024 * 1024, collective_id=0, has_side_effects=True
            ),
            cost_estimate=cost,
        )(folded, gr, gi, gb, cs, col, flip)
    gathered = lax.all_gather(folded, "mic", axis=1, tiled=True)[None]
    return pl.pallas_call(
        search_kernel,
        grid=(count,),
        in_specs=[pl.BlockSpec((1, 1, edge, edge), lambda t: (0, t, 0, 0))]
        + [whole(a) for a in (gr, gi, gb, cs, col, flip)],
        out_specs=[pl.BlockSpec((edge, edge), lambda t: (0, 0))] * 3,
        out_shape=[out] * 3,
        compiler_params=pltpu.CompilerParams(vmem_limit_bytes=40 * 1024 * 1024),
        cost_estimate=cost,
    )(gathered, gr, gi, gb, cs, col, flip)


def refine_kernel(lib_ref, ctf_ref, g_ref, cs_ref, wanted_ref, out_ref):
    step = pl.program_id(0)
    edge = ctf_ref.shape[0]

    @pl.when(step == 0)
    def _():
        out_ref[...] = jnp.full((edge, edge), -3.0e38, jnp.float32)

    @pl.when(wanted_ref[step] > 0)
    def _():
        gain = ctf_ref[...]
        fr = (lib_ref[0, :, :edge].astype(jnp.float32) * gain).astype(jnp.bfloat16).astype(jnp.float32)
        fi = (lib_ref[0, :, edge:].astype(jnp.float32) * gain).astype(jnp.bfloat16).astype(jnp.float32)
        gr = g_ref[:, :edge].astype(jnp.float32)
        gi = g_ref[:, edge:].astype(jnp.float32)
        zr = (gr * fr + gi * fi).astype(jnp.bfloat16)
        zi = (gi * fr - gr * fi).astype(jnp.bfloat16)
        ci, si = cs_ref[:, :edge], cs_ref[:, edge:]
        dot = lambda a, b: jnp.dot(a, b, preferred_element_type=jnp.float32)
        ur = (dot(ci, zr) - dot(si, zi)).astype(jnp.bfloat16)
        ui = (dot(si, zr) + dot(ci, zi)).astype(jnp.bfloat16)
        corr = dot(ur, ci) - dot(ui, si)
        out_ref[...] = jnp.maximum(out_ref[...], corr)


def refine_map(library, ctf, spectrum, cs, wanted):
    count, edge, width = library.shape
    whole = lambda a: pl.BlockSpec(a.shape, lambda t: (0, 0))
    return pl.pallas_call(
        refine_kernel,
        grid=(count,),
        in_specs=[pl.BlockSpec((1, edge, width), lambda t: (t, 0, 0))]
        + [whole(a) for a in (ctf, spectrum, cs)]
        + [pl.BlockSpec(memory_space=pltpu.SMEM)],
        out_specs=pl.BlockSpec((edge, edge), lambda t: (0, 0)),
        out_shape=jax.ShapeDtypeStruct((edge, edge), jnp.float32),
        compiler_params=pltpu.CompilerParams(vmem_limit_bytes=40 * 1024 * 1024),
        cost_estimate=pl.CostEstimate(flops=count * 700000000, bytes_accessed=count * 1200000, transcendentals=0),
    )(library, ctf, spectrum, cs, wanted)


def join(left, right):
    low = jnp.maximum(left[0], right[0].astype(jnp.float32))
    total = left[1] + right[1].astype(jnp.float32)
    square = left[2] + right[2].astype(jnp.float32)
    return (low, total, square, jnp.maximum(left[3], right[3].astype(jnp.float32)))


def merge(maps):
    size = lax.axis_size("orient")
    edge = maps[0].shape[0]
    half = edge // 2
    core = lax.axis_index("orient") % 2
    near = [(i, i ^ 1) for i in range(size)]
    narrow = lambda values: [a.astype(jnp.bfloat16) for a in values]
    mine = [lax.dynamic_slice_in_dim(a, core * half, half, 0) for a in maps]
    theirs = narrow(lax.dynamic_slice_in_dim(a, (1 - core) * half, half, 0) for a in maps)
    state = join(mine, lax.ppermute(jnp.stack(theirs), "orient", near))
    distance = 2
    while distance < size:
        far = [(i, i ^ distance) for i in range(size)]
        state = join(state, lax.ppermute(jnp.stack(narrow(state)), "orient", far))
        distance *= 2
    final = jnp.stack(narrow(state))
    other = lax.ppermute(final, "orient", near)
    first = jnp.where(core == 0, final, other)
    second = jnp.where(core == 0, other, final)
    return [jnp.concatenate([first[i], second[i]], 0).astype(jnp.float32) for i in range(4)]


def body(micrograph, search_spectra, refine_spectra, ctf, ref_owner, ref_slot):
    edge = micrograph.shape[1]
    half = edge // 2
    fwd_cos, fwd_sin, inv_cos, inv_sin = make_tables(edge)
    ctf_gain = jnp.concatenate([ctf, ctf], 1)
    rows_owned = search_spectra.shape[1]
    first_row = lax.axis_index("mic") * rows_owned
    own_gain = lax.dynamic_slice_in_dim(ctf_gain, first_row, rows_owned, 0)
    filtered = (search_spectra.astype(jnp.float32) * own_gain).astype(jnp.bfloat16)
    folded = fold_half(filtered)
    spectrum = forward(micrograph, fwd_cos, fwd_sin)

    library = refine_spectra[0]
    block_size = library.shape[0]
    ids = lax.all_gather(ref_owner[:, 0] * block_size + ref_slot[:, 0], "orient", axis=0, tiled=True)
    slots = lax.axis_index("orient") * block_size + jnp.arange(block_size, dtype=jnp.int32)
    wanted = jnp.any(slots[:, None] == ids[None, :], axis=1).astype(jnp.int32)
    cs = jnp.asarray(np.concatenate([inv_cos, inv_sin], 1))
    refined = refine_map(library, ctf, spectrum, cs, wanted)

    spec = spectrum.astype(jnp.float32)
    g_r, g_i = spec[:, :edge], spec[:, edge:]
    dc = jnp.stack([g_r[:, 0], g_i[:, 0]], 1)
    ny = jnp.stack([g_r[:, half], g_i[:, half]], 1)
    ga = (dc - ny) * 0.5
    gb = (dc + ny) * 0.5
    lane = lax.broadcasted_iota(jnp.int32, (edge, half), 1)
    h_r = jnp.where(lane == 0, ga[:, 0:1], g_r[:, :half])
    h_i = jnp.where(lane == 0, ga[:, 1:2], g_i[:, :half])
    gr = jnp.concatenate([h_r, h_r], 1)
    gi = jnp.concatenate([h_i, h_i], 1)
    sin_rows = -inv_sin[:half]
    sin_rows[0] = inv_cos[half]
    col = jnp.asarray(np.concatenate([inv_cos[:half], sin_rows], 0))
    peak, total, square = search_maps(folded, gr, gi, gb, cs, col)
    peak, total, square, refined = merge([peak, total, square, refined])
    count = float(lax.axis_size("orient") * search_spectra.shape[0])
    return (peak, total / count, peak * lax.rsqrt(square / count + 1e-05), refined)


def solution(mesh):
    in_specs = (
        P("mic", None),
        P("orient", "mic", None),
        P("mic", "orient", None, None),
        P(),
        P(("mic", "orient"), None),
        P(("mic", "orient"), None),
    )
    out_specs = (P("mic", None), P("mic", None), P("mic", None), P("mic", None))
    return jax.shard_map(body, mesh=mesh, in_specs=in_specs, out_specs=out_specs, check_vma=False)
```

```python
import functools
import math

import jax
import jax.numpy as jnp
import numpy as np
from jax import lax
from jax.experimental import pallas as pl
from jax.experimental.pallas import tpu as pltpu
from jax.sharding import PartitionSpec as P

GROUPS = 4


def make_tables(box_edge):
    positions = np.arange(box_edge, dtype=np.int32)
    products = positions[:, None] * positions[None, :] % box_edge
    angles = products.astype(np.float32) * np.float32(2.0 * math.pi / box_edge)
    cosine = np.cos(angles)
    sines = np.sin(angles)
    narrow = lambda a: a.astype(np.float32).astype(jnp.bfloat16)
    fwd_cos, fwd_sin = narrow(cosine), narrow(sines)
    inv_cos = narrow(cosine / np.float32(box_edge))
    inv_sin = narrow(sines / np.float32(box_edge))
    return (fwd_cos, fwd_sin, inv_cos, inv_sin)


def forward(tile_image, fwd_cos, fwd_sin):
    box_edge = tile_image.shape[0]
    full_map = jnp.asarray(np.concatenate([fwd_cos, fwd_sin], 1))
    halved = jnp.dot(tile_image, full_map, preferred_element_type=jnp.float32).astype(jnp.bfloat16)
    ar, ai = halved[:, :box_edge], -halved[:, box_edge:]
    stacked = jnp.concatenate(
        [jnp.concatenate([ar, ai], 1), jnp.concatenate([ai, -ar], 1)], 0
    )
    return jnp.dot(full_map, stacked, preferred_element_type=jnp.float32).astype(jnp.bfloat16)


def fold_matrices(edge):
    half = edge // 2
    mirror = np.zeros((2 * edge, edge), np.float32)
    for l in range(1, half):
        mirror[edge - l, l] = 1.0
        mirror[2 * edge - l, half + l] = -1.0
    mirror[0, 0], mirror[edge + half, 0] = 0.5, 0.5
    mirror[edge, half], mirror[half, half] = -0.5, 0.5
    row = lax.broadcasted_iota(jnp.int32, (2 * edge, edge), 0)
    col = lax.broadcasted_iota(jnp.int32, (2 * edge, edge), 1)
    own = jnp.where(row == jnp.where(col < half, col, col + half), 1.0, 0.0)
    first = jnp.where(row == 0, 0.5, jnp.where(row == edge + half, -0.5, 0.0))
    middle = jnp.where((row == edge) | (row == half), 0.5, 0.0)
    own = jnp.where(col == 0, first, jnp.where(col == half, middle, own))
    return own.astype(jnp.bfloat16), jnp.asarray(mirror, jnp.bfloat16)


def fold_half(filtered):
    count, rows, width = filtered.shape
    edge = width // 2
    mics = lax.axis_size("mic")
    own_map, mirror_map = fold_matrices(edge)
    mirrored = jnp.einsum(
        "tkc,cl->tkl", filtered, mirror_map, preferred_element_type=jnp.float32
    ).astype(jnp.bfloat16)
    flip = np.zeros((rows, rows), np.float32)
    for i in range(1, rows):
        flip[i, rows - i] = 1.0
    turned = jnp.einsum(
        "ik,tkl->til", jnp.asarray(flip, jnp.bfloat16), mirrored, preferred_element_type=jnp.float32
    ).astype(jnp.bfloat16)
    first = lax.ppermute(mirrored[:, 0, :], "mic", [(m, (mics - m) % mics) for m in range(mics)])
    rest = lax.ppermute(turned, "mic", [(m, mics - 1 - m) for m in range(mics)])
    own = jnp.einsum("tkc,cl->tkl", filtered, own_map, preferred_element_type=jnp.float32)
    row = lax.broadcasted_iota(jnp.int32, (1, rows, 1), 1)
    other = jnp.where(row == 0, first[:, None, :].astype(jnp.float32), rest.astype(jnp.float32))
    return (own + other).astype(jnp.bfloat16)


def correlate(e, gr_ref, gi_ref, gb_ref, cs_ref, col_ref, flip_ref):
    edge = gr_ref.shape[0]
    half = edge // 2
    es = jnp.concatenate([e[:, half:], e[:, :half]], axis=1)
    gr = gr_ref[...]
    gi = gi_ref[...]
    lane = lax.broadcasted_iota(jnp.int32, (edge, edge), 1)
    low = lane < half
    narrow = lax.broadcasted_iota(jnp.int32, (edge, 128), 1)
    dr = jnp.dot(
        flip_ref[...],
        jnp.where(narrow == 0, e[:, :128], pltpu.roll(es[:, :128], 1, 1)).astype(jnp.bfloat16),
        preferred_element_type=jnp.float32,
    )
    gbr, gbi = gb_ref[:, 0:1], gb_ref[:, 1:2]
    mr, mi = dr[:, 0:1], dr[:, 1:2]
    fix_r = gbr * mr - gbi * mi
    fix_i = gbr * mi + gbi * mr
    ge, ges = gr * e, gr * es
    he, hes = gi * e, gi * es
    top = jnp.where(low, ge, -ge) + hes
    bottom = ges + jnp.where(low, -he, he)
    at_r, at_i = lane == 0, lane == half
    top = top + jnp.where(at_r, fix_r, jnp.where(at_i, fix_i, 0.0))
    bottom = bottom + jnp.where(at_r, -fix_i, jnp.where(at_i, fix_r, 0.0))
    stacked = jnp.concatenate([top.astype(jnp.bfloat16), bottom.astype(jnp.bfloat16)], axis=0)
    v = jnp.dot(cs_ref[...], stacked, preferred_element_type=jnp.float32).astype(jnp.bfloat16)
    return jnp.dot(v, col_ref[...], preferred_element_type=jnp.float32)


def accumulate(corr, peak_ref, total_ref, square_ref):
    peak_ref[...] = jnp.maximum(peak_ref[...], corr)
    total_ref[...] += corr
    square_ref[...] += corr * corr


def clear(peak_ref, total_ref, square_ref):
    peak_ref[...] = jnp.full(peak_ref.shape, -3.0e38, jnp.float32)
    total_ref[...] = jnp.zeros(total_ref.shape, jnp.float32)
    square_ref[...] = jnp.zeros(square_ref.shape, jnp.float32)


def refine_correlation(template, ctf_ref, g_ref, cs_ref):
    edge = ctf_ref.shape[0]
    gain = ctf_ref[...]
    narrow = lambda a: a.astype(jnp.bfloat16)
    fr = narrow(template[:, :edge].astype(jnp.float32) * gain).astype(jnp.float32)
    fi = narrow(template[:, edge:].astype(jnp.float32) * gain).astype(jnp.float32)
    gr = g_ref[:, :edge].astype(jnp.float32)
    gi = g_ref[:, edge:].astype(jnp.float32)
    zr = narrow(gr * fr + gi * fi)
    zi = narrow(gi * fr - gr * fi)
    ci, si = cs_ref[:, :edge], cs_ref[:, edge:]
    dot = lambda a, b: jnp.dot(a, b, preferred_element_type=jnp.float32)
    ur = narrow(dot(ci, zr) - dot(si, zi))
    ui = narrow(dot(si, zr) + dot(ci, zi))
    return dot(ur, ci) - dot(ui, si)


def search_kernel(e_ref, *refs):
    @pl.when(pl.program_id(0) == 0)
    def _():
        clear(*refs[6:])

    edge = refs[0].shape[0]
    e = e_ref[...].reshape(edge, edge).astype(jnp.float32)
    accumulate(correlate(e, *refs[:6]), *refs[6:])


def remote_kernel(groups, mics, blocks, e_ref, *refs):
    operands, refine_refs = refs[:6], refs[6:10]
    maps, refined_ref = refs[10:13], refs[13]
    full, shared, up_sem, down_sem, side_sem, near_sem, far_sem, out_sem, in_sem = refs[14:]
    listed = refine_refs[0].shape[0]
    block = lax.axis_index("orient")
    edge = operands[0].shape[0]
    depth = mics // 2
    per = e_ref.shape[0] // groups
    me = lax.axis_index("mic")
    z, x = me // 2, me % 2
    above, below, beside = me + 2, me - 2, z * 2 + 1 - x
    has_above, has_below = z < depth - 1, z > 0
    mesh_id = pl.DeviceIdType.MESH
    barrier = pltpu.get_barrier_semaphore()

    @pl.when(has_above)
    def _():
        pl.semaphore_signal(barrier, inc=1, device_id={"mic": above}, device_id_type=mesh_id)

    @pl.when(has_below)
    def _():
        pl.semaphore_signal(barrier, inc=1, device_id={"mic": below}, device_id_type=mesh_id)

    pl.semaphore_signal(barrier, inc=1, device_id={"mic": beside}, device_id_type=mesh_id)
    for turn in range(1, blocks):
        pl.semaphore_signal(
            barrier,
            inc=1,
            device_id={"orient": (block + turn) % blocks},
            device_id_type=mesh_id,
        )

    full[me] = e_ref[...]
    refined_ref[...] = jnp.full(refined_ref.shape, -3.0e38, jnp.float32)
    clear(*maps)

    peers = blocks + has_above.astype(jnp.int32) + has_below.astype(jnp.int32)
    pl.semaphore_wait(barrier, peers)

    def copy(group, source, column, send_sem, recv_sem, target):
        piece = full.at[source * 2 + column, pl.ds(group * per, per)]
        slot = group * depth + source
        return pltpu.make_async_remote_copy(
            src_ref=piece,
            dst_ref=piece,
            send_sem=send_sem.at[slot],
            recv_sem=recv_sem.at[slot],
            device_id={"mic": target},
            device_id_type=mesh_id,
        )

    go_up = lambda g, source: copy(g, source, x, up_sem, near_sem, above)
    go_down = lambda g, source: copy(g, source, x, down_sem, near_sem, below)
    go_side = lambda g, source: copy(g, source, x, side_sem, far_sem, beside)
    from_side = lambda g, source: copy(g, source, 1 - x, side_sem, far_sem, beside)

    def share(turn, owner):
        return pltpu.make_async_remote_copy(
            src_ref=shared.at[owner],
            dst_ref=shared.at[owner],
            send_sem=out_sem.at[turn - 1],
            recv_sem=in_sem.at[turn - 1],
            device_id={"orient": (block + turn) % blocks},
            device_id_type=mesh_id,
        )

    def refine_one(j, carry):
        lib_ref, ctf_ref, g_ref, cap_ref = refine_refs
        corr = refine_correlation(lib_ref[j], ctf_ref, g_ref, operands[3])
        refined_ref[...] = jnp.maximum(refined_ref[...], jnp.minimum(corr, cap_ref[j]))
        return carry

    for step in range(groups + depth):
        for hop in range(depth):
            g = step - hop
            if g < 0 or g >= groups:
                continue
            if hop == 0:

                @pl.when(has_above)
                def _(g=g):
                    go_up(g, z).start()

                @pl.when(has_below)
                def _(g=g):
                    go_down(g, z).start()

                go_side(g, z).start()
                continue

            @pl.when(z - hop >= 0)
            def _(g=g, hop=hop):
                go_up(g, z - hop).wait_recv()

                @pl.when(has_above)
                def _():
                    go_up(g, z - hop).start()

                go_side(g, z - hop).start()

            @pl.when(z + hop < depth)
            def _(g=g, hop=hop):
                go_down(g, z + hop).wait_recv()

                @pl.when(has_below)
                def _():
                    go_down(g, z + hop).start()

                go_side(g, z + hop).start()

        if step < depth:
            lax.fori_loop(step * listed // depth, (step + 1) * listed // depth, refine_one, 0)
        if step == depth - 1:
            shared[block] = refined_ref[...].astype(jnp.bfloat16)
            for turn in range(1, blocks):
                share(turn, block).start()

        g = step - depth
        if g >= 0:
            for source in range(depth):
                from_side(g, source).wait_recv()

            def one(t, carry):
                e = full[:, t].reshape(edge, edge).astype(jnp.float32)
                accumulate(correlate(e, *operands), *maps)
                return carry

            lax.fori_loop(g * per, (g + 1) * per, one, 0)

    for turn in range(1, blocks):
        owner = (block + blocks - turn) % blocks
        share(turn, owner).wait_recv()
        refined_ref[...] = jnp.maximum(refined_ref[...], shared[owner].astype(jnp.float32))
    for turn in range(1, blocks):
        share(turn, block).wait_send()

    for g in range(groups):
        for source in range(depth):
            go_side(g, source).wait_send()

            @pl.when(jnp.logical_and(has_above, z >= source))
            def _(g=g, source=source):
                go_up(g, source).wait_send()

            @pl.when(jnp.logical_and(has_below, z <= source))
            def _(g=g, source=source):
                go_down(g, source).wait_send()


def all_maps(folded, gr, gi, gb, cs, col, library, ctf, spectrum, wanted):
    count, rows, edge = folded.shape
    mics = lax.axis_size("mic")
    place = lambda axis: lax.broadcasted_iota(jnp.int32, (edge, edge), axis)
    flip = ((place(0) + place(1)) % edge == 0).astype(jnp.bfloat16)
    whole = lambda a: pl.BlockSpec(a.shape, lambda t: (0, 0))
    out = jax.ShapeDtypeStruct((edge, edge), jnp.float32)
    cost = pl.CostEstimate(
        flops=count * 350000000, bytes_accessed=count * 600000, transcendentals=0
    )
    if rows % 16 == 0 and mics % 2 == 0:
        groups = GROUPS if count % GROUPS == 0 else 1
        slots = groups * (mics // 2)
        blocks = lax.axis_size("orient")
        cap = jnp.where(wanted > 0, 3.0e38, -3.0e38).astype(jnp.float32)
        cap = jnp.broadcast_to(cap[:, None, None], (wanted.shape[0], 1, edge))
        vmem = pl.BlockSpec(memory_space=pltpu.VMEM)
        *maps, refined = pl.pallas_call(
            functools.partial(remote_kernel, groups, mics, blocks),
            in_specs=[vmem] * 11,
            out_specs=[vmem] * 4,
            out_shape=[out] * 4,
            scratch_shapes=[
                pltpu.VMEM((mics, count, rows, edge), jnp.bfloat16),
                pltpu.VMEM((blocks, edge, edge), jnp.bfloat16),
            ]
            + [pltpu.SemaphoreType.DMA((slots,))] * 5
            + [pltpu.SemaphoreType.DMA((blocks - 1,))] * 2,
            compiler_params=pltpu.CompilerParams(
                vmem_limit_bytes=40 * 1024 * 1024, collective_id=0, has_side_effects=True
            ),
            cost_estimate=cost,
        )(folded, gr, gi, gb, cs, col, flip, library, ctf, spectrum, cap)
        return merge(maps) + [refined]
    refined = refine_map(library, ctf, spectrum, cs, wanted)
    gathered = lax.all_gather(folded, "mic", axis=1, tiled=True)[None]
    maps = pl.pallas_call(
        search_kernel,
        grid=(count,),
        in_specs=[pl.BlockSpec((1, 1, edge, edge), lambda t: (0, t, 0, 0))]
        + [whole(a) for a in (gr, gi, gb, cs, col, flip)],
        out_specs=[pl.BlockSpec((edge, edge), lambda t: (0, 0))] * 3,
        out_shape=[out] * 3,
        compiler_params=pltpu.CompilerParams(vmem_limit_bytes=40 * 1024 * 1024),
        cost_estimate=cost,
    )(gathered, gr, gi, gb, cs, col, flip)
    return merge([*maps, refined])


def refine_kernel(lib_ref, ctf_ref, g_ref, cs_ref, wanted_ref, out_ref):
    step = pl.program_id(0)
    edge = ctf_ref.shape[0]

    @pl.when(step == 0)
    def _():
        out_ref[...] = jnp.full((edge, edge), -3.0e38, jnp.float32)

    @pl.when(wanted_ref[step] > 0)
    def _():
        corr = refine_correlation(lib_ref[0], ctf_ref, g_ref, cs_ref)
        out_ref[...] = jnp.maximum(out_ref[...], corr)


def refine_map(library, ctf, spectrum, cs, wanted):
    count, edge, width = library.shape
    whole = lambda a: pl.BlockSpec(a.shape, lambda t: (0, 0))
    return pl.pallas_call(
        refine_kernel,
        grid=(count,),
        in_specs=[pl.BlockSpec((1, edge, width), lambda t: (t, 0, 0))]
        + [whole(a) for a in (ctf, spectrum, cs)]
        + [pl.BlockSpec(memory_space=pltpu.SMEM)],
        out_specs=pl.BlockSpec((edge, edge), lambda t: (0, 0)),
        out_shape=jax.ShapeDtypeStruct((edge, edge), jnp.float32),
        compiler_params=pltpu.CompilerParams(vmem_limit_bytes=40 * 1024 * 1024),
        cost_estimate=pl.CostEstimate(flops=count * 700000000, bytes_accessed=count * 1200000, transcendentals=0),
    )(library, ctf, spectrum, cs, wanted)


def join(left, right):
    right = [a.astype(jnp.float32) for a in right]
    return [
        jnp.maximum(a, b) if i in (0, 3) else a + b for i, (a, b) in enumerate(zip(left, right))
    ]


def merge(maps):
    size = lax.axis_size("orient")
    edge = maps[0].shape[0]
    half = edge // 2
    core = lax.axis_index("orient") % 2
    near = [(i, i ^ 1) for i in range(size)]
    narrow = lambda values: [a.astype(jnp.bfloat16) for a in values]
    mine = [lax.dynamic_slice_in_dim(a, core * half, half, 0) for a in maps]
    theirs = narrow(lax.dynamic_slice_in_dim(a, (1 - core) * half, half, 0) for a in maps)
    state = join(mine, lax.ppermute(jnp.stack(theirs), "orient", near))
    distance = 2
    while distance < size:
        far = [(i, i ^ distance) for i in range(size)]
        state = join(state, lax.ppermute(jnp.stack(narrow(state)), "orient", far))
        distance *= 2
    final = jnp.stack(narrow(state))
    other = lax.ppermute(final, "orient", near)
    first = jnp.where(core == 0, final, other)
    second = jnp.where(core == 0, other, final)
    return [jnp.concatenate([first[i], second[i]], 0).astype(jnp.float32) for i in range(len(maps))]


def body(micrograph, search_spectra, refine_spectra, ctf, ref_owner, ref_slot):
    edge = micrograph.shape[1]
    half = edge // 2
    fwd_cos, fwd_sin, inv_cos, inv_sin = make_tables(edge)
    ctf_gain = jnp.concatenate([ctf, ctf], 1)
    rows_owned = search_spectra.shape[1]
    first_row = lax.axis_index("mic") * rows_owned
    own_gain = lax.dynamic_slice_in_dim(ctf_gain, first_row, rows_owned, 0)
    filtered = (search_spectra.astype(jnp.float32) * own_gain).astype(jnp.bfloat16)
    folded = fold_half(filtered)
    spectrum = forward(micrograph, fwd_cos, fwd_sin)

    library = refine_spectra[0]
    block_size = library.shape[0]
    ids = lax.all_gather(ref_owner[:, 0] * block_size + ref_slot[:, 0], "orient", axis=0, tiled=True)
    slots = lax.axis_index("orient") * block_size + jnp.arange(block_size, dtype=jnp.int32)
    wanted = jnp.any(slots[:, None] == ids[None, :], axis=1).astype(jnp.int32)
    cs = jnp.asarray(np.concatenate([inv_cos, inv_sin], 1))

    spec = spectrum.astype(jnp.float32)
    g_r, g_i = spec[:, :edge], spec[:, edge:]
    dc = jnp.stack([g_r[:, 0], g_i[:, 0]], 1)
    ny = jnp.stack([g_r[:, half], g_i[:, half]], 1)
    ga = (dc - ny) * 0.5
    gb = (dc + ny) * 0.5
    lane = lax.broadcasted_iota(jnp.int32, (edge, half), 1)
    h_r = jnp.where(lane == 0, ga[:, 0:1], g_r[:, :half])
    h_i = jnp.where(lane == 0, ga[:, 1:2], g_i[:, :half])
    gr = jnp.concatenate([h_r, h_r], 1)
    gi = jnp.concatenate([h_i, h_i], 1)
    sin_rows = -inv_sin[:half]
    sin_rows[0] = inv_cos[half]
    col = jnp.asarray(np.concatenate([inv_cos[:half], sin_rows], 0))
    peak, total, square, refined = all_maps(
        folded, gr, gi, gb, cs, col, library, ctf, spectrum, wanted
    )
    count = float(lax.axis_size("orient") * search_spectra.shape[0])
    return (peak, total / count, peak * lax.rsqrt(square / count + 1e-05), refined)


def solution(mesh):
    in_specs = (
        P("mic", None),
        P("orient", "mic", None),
        P("mic", "orient", None, None),
        P(),
        P(("mic", "orient"), None),
        P(("mic", "orient"), None),
    )
    out_specs = (P("mic", None), P("mic", None), P("mic", None), P("mic", None))
    return jax.shard_map(body, mesh=mesh, in_specs=in_specs, out_specs=out_specs, check_vma=False)
```

```python
import functools
import math

import jax
import jax.numpy as jnp
import numpy as np
from jax import lax
from jax.experimental import pallas as pl
from jax.experimental.pallas import tpu as pltpu
from jax.sharding import PartitionSpec as P

GROUPS = 4


def make_tables(box_edge):
    positions = np.arange(box_edge, dtype=np.int32)
    products = positions[:, None] * positions[None, :] % box_edge
    angles = products.astype(np.float32) * np.float32(2.0 * math.pi / box_edge)
    cosine = np.cos(angles)
    sines = np.sin(angles)
    narrow = lambda a: a.astype(np.float32).astype(jnp.bfloat16)
    fwd_cos, fwd_sin = narrow(cosine), narrow(sines)
    inv_cos = narrow(cosine / np.float32(box_edge))
    inv_sin = narrow(sines / np.float32(box_edge))
    return (fwd_cos, fwd_sin, inv_cos, inv_sin)


def forward(tile_image, fwd_cos, fwd_sin):
    box_edge = tile_image.shape[0]
    full_map = jnp.asarray(np.concatenate([fwd_cos, fwd_sin], 1))
    halved = jnp.dot(tile_image, full_map, preferred_element_type=jnp.float32).astype(jnp.bfloat16)
    ar, ai = halved[:, :box_edge], -halved[:, box_edge:]
    stacked = jnp.concatenate(
        [jnp.concatenate([ar, ai], 1), jnp.concatenate([ai, -ar], 1)], 0
    )
    return jnp.dot(full_map, stacked, preferred_element_type=jnp.float32).astype(jnp.bfloat16)


def fold_matrices(edge):
    half = edge // 2
    mirror = np.zeros((2 * edge, edge), np.float32)
    for l in range(1, half):
        mirror[edge - l, l] = 1.0
        mirror[2 * edge - l, half + l] = -1.0
    mirror[0, 0], mirror[edge + half, 0] = 0.5, 0.5
    mirror[edge, half], mirror[half, half] = -0.5, 0.5
    row = lax.broadcasted_iota(jnp.int32, (2 * edge, edge), 0)
    col = lax.broadcasted_iota(jnp.int32, (2 * edge, edge), 1)
    own = jnp.where(row == jnp.where(col < half, col, col + half), 1.0, 0.0)
    first = jnp.where(row == 0, 0.5, jnp.where(row == edge + half, -0.5, 0.0))
    middle = jnp.where((row == edge) | (row == half), 0.5, 0.0)
    own = jnp.where(col == 0, first, jnp.where(col == half, middle, own))
    return own.astype(jnp.bfloat16), jnp.asarray(mirror, jnp.bfloat16)


def fold_half(filtered):
    count, rows, width = filtered.shape
    edge = width // 2
    mics = lax.axis_size("mic")
    own_map, mirror_map = fold_matrices(edge)
    mirrored = jnp.einsum(
        "tkc,cl->tkl", filtered, mirror_map, preferred_element_type=jnp.float32
    ).astype(jnp.bfloat16)
    flip = np.zeros((rows, rows), np.float32)
    for i in range(1, rows):
        flip[i, rows - i] = 1.0
    turned = jnp.einsum(
        "ik,tkl->til", jnp.asarray(flip, jnp.bfloat16), mirrored, preferred_element_type=jnp.float32
    ).astype(jnp.bfloat16)
    first = lax.ppermute(mirrored[:, 0, :], "mic", [(m, (mics - m) % mics) for m in range(mics)])
    own = jnp.einsum("tkc,cl->tkl", filtered, own_map, preferred_element_type=jnp.float32)
    row = lax.broadcasted_iota(jnp.int32, (1, rows, 1), 1)
    own = own + jnp.where(row == 0, first[:, None, :].astype(jnp.float32), 0.0)
    return own.astype(jnp.bfloat16), turned


def correlate(e, gr_ref, gi_ref, gb_ref, cs_ref, col_ref, flip_ref):
    edge = gr_ref.shape[0]
    half = edge // 2
    es = jnp.concatenate([e[:, half:], e[:, :half]], axis=1)
    gr = gr_ref[...]
    gi = gi_ref[...]
    lane = lax.broadcasted_iota(jnp.int32, (edge, edge), 1)
    low = lane < half
    narrow = lax.broadcasted_iota(jnp.int32, (edge, 128), 1)
    dr = jnp.dot(
        flip_ref[...],
        jnp.where(narrow == 0, e[:, :128], pltpu.roll(es[:, :128], 1, 1)).astype(jnp.bfloat16),
        preferred_element_type=jnp.float32,
    )
    gbr, gbi = gb_ref[:, 0:1], gb_ref[:, 1:2]
    mr, mi = dr[:, 0:1], dr[:, 1:2]
    fix_r = gbr * mr - gbi * mi
    fix_i = gbr * mi + gbi * mr
    ge, ges = gr * e, gr * es
    he, hes = gi * e, gi * es
    top = jnp.where(low, ge, -ge) + hes
    bottom = ges + jnp.where(low, -he, he)
    at_r, at_i = lane == 0, lane == half
    top = top + jnp.where(at_r, fix_r, jnp.where(at_i, fix_i, 0.0))
    bottom = bottom + jnp.where(at_r, -fix_i, jnp.where(at_i, fix_r, 0.0))
    stacked = jnp.concatenate([top.astype(jnp.bfloat16), bottom.astype(jnp.bfloat16)], axis=0)
    v = jnp.dot(cs_ref[...], stacked, preferred_element_type=jnp.float32).astype(jnp.bfloat16)
    return jnp.dot(v, col_ref[...], preferred_element_type=jnp.float32)


def accumulate(corr, peak_ref, total_ref, square_ref):
    peak_ref[...] = jnp.maximum(peak_ref[...], corr)
    total_ref[...] += corr
    square_ref[...] += corr * corr


def clear(peak_ref, total_ref, square_ref):
    peak_ref[...] = jnp.full(peak_ref.shape, -3.0e38, jnp.float32)
    total_ref[...] = jnp.zeros(total_ref.shape, jnp.float32)
    square_ref[...] = jnp.zeros(square_ref.shape, jnp.float32)


def refine_correlation(template, ctf_ref, g_ref, cs_ref):
    edge = ctf_ref.shape[0]
    gain = ctf_ref[...]
    narrow = lambda a: a.astype(jnp.bfloat16)
    fr = narrow(template[:, :edge].astype(jnp.float32) * gain).astype(jnp.float32)
    fi = narrow(template[:, edge:].astype(jnp.float32) * gain).astype(jnp.float32)
    gr = g_ref[:, :edge].astype(jnp.float32)
    gi = g_ref[:, edge:].astype(jnp.float32)
    zr = narrow(gr * fr + gi * fi)
    zi = narrow(gi * fr - gr * fi)
    ci, si = cs_ref[:, :edge], cs_ref[:, edge:]
    dot = lambda a, b: jnp.dot(a, b, preferred_element_type=jnp.float32)
    ur = narrow(dot(ci, zr) - dot(si, zi))
    ui = narrow(dot(si, zr) + dot(ci, zi))
    return dot(ur, ci) - dot(ui, si)


def search_kernel(e_ref, *refs):
    @pl.when(pl.program_id(0) == 0)
    def _():
        clear(*refs[6:])

    edge = refs[0].shape[0]
    e = e_ref[...].reshape(edge, edge).astype(jnp.float32)
    accumulate(correlate(e, *refs[:6]), *refs[6:])


def remote_kernel(groups, mics, blocks, e_ref, turned_ref, *refs):
    operands, refine_refs = refs[:6], refs[6:10]
    maps, refined_ref = refs[10:13], refs[13]
    full, shared, mirror, up_sem, down_sem, side_sem, near_sem, far_sem = refs[14:22]
    out_sem, in_sem, there_sem, back_sem = refs[22:]
    listed = refine_refs[0].shape[0]
    block = lax.axis_index("orient")
    edge = operands[0].shape[0]
    depth = mics // 2
    per = e_ref.shape[0] // groups
    me = lax.axis_index("mic")
    z, x = me // 2, me % 2
    above, below, beside = me + 2, me - 2, z * 2 + 1 - x
    has_above, has_below = z < depth - 1, z > 0
    mesh_id = pl.DeviceIdType.MESH
    barrier = pltpu.get_barrier_semaphore()

    @pl.when(has_above)
    def _():
        pl.semaphore_signal(barrier, inc=1, device_id={"mic": above}, device_id_type=mesh_id)

    @pl.when(has_below)
    def _():
        pl.semaphore_signal(barrier, inc=1, device_id={"mic": below}, device_id_type=mesh_id)

    pl.semaphore_signal(barrier, inc=1, device_id={"mic": beside}, device_id_type=mesh_id)
    for turn in range(1, blocks):
        pl.semaphore_signal(
            barrier,
            inc=1,
            device_id={"orient": (block + turn) % blocks},
            device_id_type=mesh_id,
        )

    opposite = mics - 1 - me
    pl.semaphore_signal(barrier, inc=1, device_id={"mic": opposite}, device_id_type=mesh_id)
    refined_ref[...] = jnp.full(refined_ref.shape, -3.0e38, jnp.float32)
    clear(*maps)

    peers = 1 + blocks + has_above.astype(jnp.int32) + has_below.astype(jnp.int32)
    pl.semaphore_wait(barrier, peers)

    def copy(group, source, column, send_sem, recv_sem, target):
        piece = full.at[source * 2 + column, pl.ds(group * per, per)]
        slot = group * depth + source
        return pltpu.make_async_remote_copy(
            src_ref=piece,
            dst_ref=piece,
            send_sem=send_sem.at[slot],
            recv_sem=recv_sem.at[slot],
            device_id={"mic": target},
            device_id_type=mesh_id,
        )

    go_up = lambda g, source: copy(g, source, x, up_sem, near_sem, above)
    go_down = lambda g, source: copy(g, source, x, down_sem, near_sem, below)
    go_side = lambda g, source: copy(g, source, x, side_sem, far_sem, beside)
    from_side = lambda g, source: copy(g, source, 1 - x, side_sem, far_sem, beside)

    def share(turn, owner):
        return pltpu.make_async_remote_copy(
            src_ref=shared.at[owner],
            dst_ref=shared.at[owner],
            send_sem=out_sem.at[turn - 1],
            recv_sem=in_sem.at[turn - 1],
            device_id={"orient": (block + turn) % blocks},
            device_id_type=mesh_id,
        )

    def refine_one(j, carry):
        lib_ref, ctf_ref, g_ref, cap_ref = refine_refs
        corr = refine_correlation(lib_ref[j], ctf_ref, g_ref, operands[3])
        refined_ref[...] = jnp.maximum(refined_ref[...], jnp.minimum(corr, cap_ref[j]))
        return carry

    def swap(g):
        rows = pl.ds(g * per, per)
        return pltpu.make_async_remote_copy(
            src_ref=turned_ref.at[rows],
            dst_ref=mirror.at[rows],
            send_sem=there_sem.at[g],
            recv_sem=back_sem.at[g],
            device_id={"mic": opposite},
            device_id_type=mesh_id,
        )

    for g in range(min(2, groups)):
        swap(g).start()

    for step in range(groups + depth):
        for hop in range(depth):
            g = step - hop
            if g < 0 or g >= groups:
                continue
            if hop == 0:
                swap(g).wait_recv()
                if g + 2 < groups:
                    swap(g + 2).start()
                rows = pl.ds(g * per, per)
                both = e_ref[rows].astype(jnp.float32) + mirror[rows].astype(jnp.float32)
                full[me, rows] = both.astype(jnp.bfloat16)

                @pl.when(has_above)
                def _(g=g):
                    go_up(g, z).start()

                @pl.when(has_below)
                def _(g=g):
                    go_down(g, z).start()

                go_side(g, z).start()
                continue

            @pl.when(z - hop >= 0)
            def _(g=g, hop=hop):
                go_up(g, z - hop).wait_recv()

                @pl.when(has_above)
                def _():
                    go_up(g, z - hop).start()

                go_side(g, z - hop).start()

            @pl.when(z + hop < depth)
            def _(g=g, hop=hop):
                go_down(g, z + hop).wait_recv()

                @pl.when(has_below)
                def _():
                    go_down(g, z + hop).start()

                go_side(g, z + hop).start()

        if step < depth:
            lax.fori_loop(step * listed // depth, (step + 1) * listed // depth, refine_one, 0)
        if step == depth - 1:
            shared[block] = refined_ref[...].astype(jnp.bfloat16)
            for turn in range(1, blocks):
                share(turn, block).start()

        g = step - depth
        if g >= 0:
            for source in range(depth):
                from_side(g, source).wait_recv()

            def one(t, carry):
                e = full[:, t].reshape(edge, edge).astype(jnp.float32)
                accumulate(correlate(e, *operands), *maps)
                return carry

            lax.fori_loop(g * per, (g + 1) * per, one, 0)

    for turn in range(1, blocks):
        owner = (block + blocks - turn) % blocks
        share(turn, owner).wait_recv()
        refined_ref[...] = jnp.maximum(refined_ref[...], shared[owner].astype(jnp.float32))
    for turn in range(1, blocks):
        share(turn, block).wait_send()
    for g in range(groups):
        swap(g).wait_send()

    for g in range(groups):
        for source in range(depth):
            go_side(g, source).wait_send()

            @pl.when(jnp.logical_and(has_above, z >= source))
            def _(g=g, source=source):
                go_up(g, source).wait_send()

            @pl.when(jnp.logical_and(has_below, z <= source))
            def _(g=g, source=source):
                go_down(g, source).wait_send()


def all_maps(folded, turned, gr, gi, gb, cs, col, library, ctf, spectrum, wanted):
    count, rows, edge = folded.shape
    mics = lax.axis_size("mic")
    place = lambda axis: lax.broadcasted_iota(jnp.int32, (edge, edge), axis)
    flip = ((place(0) + place(1)) % edge == 0).astype(jnp.bfloat16)
    whole = lambda a: pl.BlockSpec(a.shape, lambda t: (0, 0))
    out = jax.ShapeDtypeStruct((edge, edge), jnp.float32)
    cost = pl.CostEstimate(
        flops=count * 350000000, bytes_accessed=count * 600000, transcendentals=0
    )
    if rows % 16 == 0 and mics % 2 == 0:
        groups = GROUPS if count % GROUPS == 0 else 1
        slots = groups * (mics // 2)
        blocks = lax.axis_size("orient")
        cap = jnp.where(wanted > 0, 3.0e38, -3.0e38).astype(jnp.float32)
        cap = jnp.broadcast_to(cap[:, None, None], (wanted.shape[0], 1, edge))
        vmem = pl.BlockSpec(memory_space=pltpu.VMEM)
        *maps, refined = pl.pallas_call(
            functools.partial(remote_kernel, groups, mics, blocks),
            in_specs=[vmem] * 12,
            out_specs=[vmem] * 4,
            out_shape=[out] * 4,
            scratch_shapes=[
                pltpu.VMEM((mics, count, rows, edge), jnp.bfloat16),
                pltpu.VMEM((blocks, edge, edge), jnp.bfloat16),
                pltpu.VMEM((count, rows, edge), jnp.bfloat16),
            ]
            + [pltpu.SemaphoreType.DMA((slots,))] * 5
            + [pltpu.SemaphoreType.DMA((blocks - 1,))] * 2
            + [pltpu.SemaphoreType.DMA((groups,))] * 2,
            compiler_params=pltpu.CompilerParams(
                vmem_limit_bytes=40 * 1024 * 1024, collective_id=0, has_side_effects=True
            ),
            cost_estimate=cost,
        )(folded, turned, gr, gi, gb, cs, col, flip, library, ctf, spectrum, cap)
        return merge(maps) + [refined]
    refined = refine_map(library, ctf, spectrum, cs, wanted)
    rest = lax.ppermute(turned, "mic", [(m, mics - 1 - m) for m in range(mics)])
    folded = (folded.astype(jnp.float32) + rest.astype(jnp.float32)).astype(jnp.bfloat16)
    gathered = lax.all_gather(folded, "mic", axis=1, tiled=True)[None]
    maps = pl.pallas_call(
        search_kernel,
        grid=(count,),
        in_specs=[pl.BlockSpec((1, 1, edge, edge), lambda t: (0, t, 0, 0))]
        + [whole(a) for a in (gr, gi, gb, cs, col, flip)],
        out_specs=[pl.BlockSpec((edge, edge), lambda t: (0, 0))] * 3,
        out_shape=[out] * 3,
        compiler_params=pltpu.CompilerParams(vmem_limit_bytes=40 * 1024 * 1024),
        cost_estimate=cost,
    )(gathered, gr, gi, gb, cs, col, flip)
    return merge([*maps, refined])


def refine_kernel(lib_ref, ctf_ref, g_ref, cs_ref, wanted_ref, out_ref):
    step = pl.program_id(0)
    edge = ctf_ref.shape[0]

    @pl.when(step == 0)
    def _():
        out_ref[...] = jnp.full((edge, edge), -3.0e38, jnp.float32)

    @pl.when(wanted_ref[step] > 0)
    def _():
        corr = refine_correlation(lib_ref[0], ctf_ref, g_ref, cs_ref)
        out_ref[...] = jnp.maximum(out_ref[...], corr)


def refine_map(library, ctf, spectrum, cs, wanted):
    count, edge, width = library.shape
    whole = lambda a: pl.BlockSpec(a.shape, lambda t: (0, 0))
    return pl.pallas_call(
        refine_kernel,
        grid=(count,),
        in_specs=[pl.BlockSpec((1, edge, width), lambda t: (t, 0, 0))]
        + [whole(a) for a in (ctf, spectrum, cs)]
        + [pl.BlockSpec(memory_space=pltpu.SMEM)],
        out_specs=pl.BlockSpec((edge, edge), lambda t: (0, 0)),
        out_shape=jax.ShapeDtypeStruct((edge, edge), jnp.float32),
        compiler_params=pltpu.CompilerParams(vmem_limit_bytes=40 * 1024 * 1024),
        cost_estimate=pl.CostEstimate(flops=count * 700000000, bytes_accessed=count * 1200000, transcendentals=0),
    )(library, ctf, spectrum, cs, wanted)


def join(left, right):
    right = [a.astype(jnp.float32) for a in right]
    return [
        jnp.maximum(a, b) if i in (0, 3) else a + b for i, (a, b) in enumerate(zip(left, right))
    ]


def merge(maps):
    size = lax.axis_size("orient")
    edge = maps[0].shape[0]
    half = edge // 2
    core = lax.axis_index("orient") % 2
    near = [(i, i ^ 1) for i in range(size)]
    narrow = lambda values: [a.astype(jnp.bfloat16) for a in values]
    mine = [lax.dynamic_slice_in_dim(a, core * half, half, 0) for a in maps]
    theirs = narrow(lax.dynamic_slice_in_dim(a, (1 - core) * half, half, 0) for a in maps)
    state = join(mine, lax.ppermute(jnp.stack(theirs), "orient", near))
    distance = 2
    while distance < size:
        far = [(i, i ^ distance) for i in range(size)]
        state = join(state, lax.ppermute(jnp.stack(narrow(state)), "orient", far))
        distance *= 2
    final = jnp.stack(narrow(state))
    other = lax.ppermute(final, "orient", near)
    first = jnp.where(core == 0, final, other)
    second = jnp.where(core == 0, other, final)
    return [jnp.concatenate([first[i], second[i]], 0).astype(jnp.float32) for i in range(len(maps))]


def body(micrograph, search_spectra, refine_spectra, ctf, ref_owner, ref_slot):
    edge = micrograph.shape[1]
    half = edge // 2
    fwd_cos, fwd_sin, inv_cos, inv_sin = make_tables(edge)
    ctf_gain = jnp.concatenate([ctf, ctf], 1)
    rows_owned = search_spectra.shape[1]
    first_row = lax.axis_index("mic") * rows_owned
    own_gain = lax.dynamic_slice_in_dim(ctf_gain, first_row, rows_owned, 0)
    filtered = (search_spectra.astype(jnp.float32) * own_gain).astype(jnp.bfloat16)
    folded, turned = fold_half(filtered)
    spectrum = forward(micrograph, fwd_cos, fwd_sin)

    library = refine_spectra[0]
    block_size = library.shape[0]
    ids = lax.all_gather(ref_owner[:, 0] * block_size + ref_slot[:, 0], "orient", axis=0, tiled=True)
    slots = lax.axis_index("orient") * block_size + jnp.arange(block_size, dtype=jnp.int32)
    wanted = jnp.any(slots[:, None] == ids[None, :], axis=1).astype(jnp.int32)
    cs = jnp.asarray(np.concatenate([inv_cos, inv_sin], 1))

    spec = spectrum.astype(jnp.float32)
    g_r, g_i = spec[:, :edge], spec[:, edge:]
    dc = jnp.stack([g_r[:, 0], g_i[:, 0]], 1)
    ny = jnp.stack([g_r[:, half], g_i[:, half]], 1)
    ga = (dc - ny) * 0.5
    gb = (dc + ny) * 0.5
    lane = lax.broadcasted_iota(jnp.int32, (edge, half), 1)
    h_r = jnp.where(lane == 0, ga[:, 0:1], g_r[:, :half])
    h_i = jnp.where(lane == 0, ga[:, 1:2], g_i[:, :half])
    gr = jnp.concatenate([h_r, h_r], 1)
    gi = jnp.concatenate([h_i, h_i], 1)
    sin_rows = -inv_sin[:half]
    sin_rows[0] = inv_cos[half]
    col = jnp.asarray(np.concatenate([inv_cos[:half], sin_rows], 0))
    peak, total, square, refined = all_maps(
        folded, turned, gr, gi, gb, cs, col, library, ctf, spectrum, wanted
    )
    count = float(lax.axis_size("orient") * search_spectra.shape[0])
    return (peak, total / count, peak * lax.rsqrt(square / count + 1e-05), refined)


def solution(mesh):
    in_specs = (
        P("mic", None),
        P("orient", "mic", None),
        P("mic", "orient", None, None),
        P(),
        P(("mic", "orient"), None),
        P(("mic", "orient"), None),
    )
    out_specs = (P("mic", None), P("mic", None), P("mic", None), P("mic", None))
    return jax.shard_map(body, mesh=mesh, in_specs=in_specs, out_specs=out_specs, check_vma=False)
```
